32 devices in a mesh: beam: 2 (over x), band: 2 (over core), tm: 8 (over z, y).
Axes of the slice: x: 2, y: 2, z: 4, core: 2. Of those that a mesh axis runs over, the one named last changes fastest.
Arguments:
- samples: bfloat16 [2048, 32768], P(('beam', 'band'), 'tm'), parts along dimension 0, may hold values from -3 to 3
- clip_mask: int32 [2048, 256], P(('beam', 'band'), 'tm'), parts along dimension 0, may hold values 0 or 1
- delays: int32 [8, 1024], P(None, 'band'), may hold values from 0 to 4095
- templates: bfloat16 [2, 64, 1024], replicated, may hold values from -0.125 to 0.125
Outputs:
- powers: float32 [16, 64, 16384], P(('beam', 'tm'), None, 'band'), parts along dimension 0
The draws below stay inside these ranges and needn't reach their ends.
There are 2 independent parts, one for each index of `beam`. The reference program is written for one: setup_inputs(seed, part) draws one part's arguments, and reference() takes and returns one part's arrays. A program takes and returns all parts, laid end to end along the dimension named above; an argument that names none is the same for every part. Nothing has to cross between parts.
All inputs are finite; a program needn't handle non-finite values. No bound on the sum of `clip_mask` on one device may be relied on, other than what follows from the above.
Results may differ from the reference program's by a relative error of at most 0.0095.
Values may be sent and summed in bfloat16 or wider, within the bound.
A program may use at most 192 MiB of HBM per device.

```python
import math
import jax
import jax.numpy as jnp
from jax import lax

CHANNELS = 1024
FFT_LEN = 8192
TEMPLATES = 64
TEMPLATE_LEN = 1024
FLAG_SPAN = 128
SEARCH = 16384
SLAB = 4096
SAMPLES = 32768
DMS = 8
N_TM = 8


def draw_samples(key, part):
    noise_key = jax.random.fold_in(key, 11)
    step_key = jax.random.fold_in(key, 12)
    offset_key = jax.random.fold_in(key, 13)
    lowest_step = 15 * FFT_LEN // 100
    highest_step = 48 * FFT_LEN // 100
    tone_steps = jax.random.randint(step_key, (CHANNELS, 1), lowest_step, highest_step, dtype=jnp.int32)
    offsets = jax.random.randint(offset_key, (CHANNELS, 1), 0, FFT_LEN, dtype=jnp.int32)
    sample_index = jnp.arange(SAMPLES, dtype=jnp.int32) % FFT_LEN
    turn_count = (sample_index[None, :] * tone_steps + offsets) % FFT_LEN
    angles = turn_count.astype(jnp.float32) * (2.0 * math.pi / FFT_LEN)
    tone_wave = jnp.sin(angles)
    noise_part = 0.2 * jax.random.truncated_normal(noise_key, -3.0, 3.0, (CHANNELS, SAMPLES), jnp.float32)
    amplitude = 2.0
    return (amplitude * tone_wave + noise_part).astype(jnp.bfloat16)


def place_ends(values, key, smallest, high):
    place = [jax.random.randint(jax.random.fold_in(key, axis), (), 0, length) for axis, length in enumerate(values.shape)]
    main_axis = values.shape.index(max(values.shape))
    beside = place[:main_axis] + [(place[main_axis] + 1) % values.shape[main_axis]] + place[main_axis + 1:]
    return values.at[tuple(place)].set(smallest).at[tuple(beside)].set(high)


def noise(key, extent, deviation, most, kind=jnp.bfloat16):
    entries = deviation * jax.random.normal(key, extent, jnp.float32)
    return jnp.clip(entries, min=-most, max=most).astype(kind)


def setup_inputs(seed: int = 0, part: int = 0) -> dict:
    arg_keys = jax.random.split(jax.random.key(seed), 5)
    part_keys = jax.random.split(jax.random.fold_in(arg_keys[4], part), 5)
    return {
        "samples": draw_samples(jax.random.fold_in(jax.random.fold_in(arg_keys[4], part), 71), part),
        "clip_mask": place_ends((jax.random.randint(part_keys[1], (CHANNELS, SAMPLES // FLAG_SPAN), 0, 8) < 7).astype(jnp.int32), jax.random.fold_in(part_keys[1], 1), 0, 1),
        "delays": place_ends(jax.random.randint(arg_keys[2], (DMS, CHANNELS), 0, SLAB), jax.random.fold_in(arg_keys[2], 1), 0, SLAB - 1).astype(jnp.int32),
        "templates": noise(arg_keys[3], (2, TEMPLATES, TEMPLATE_LEN), (2 * TEMPLATE_LEN) ** -0.5, 0.125),
    }


clip_level = 2.5
highest = lax.Precision.HIGHEST

def reference(samples, clip_mask, delays, templates):
    widened = jnp.repeat(clip_mask, FLAG_SPAN, axis=1).astype(jnp.float32)
    cleaned = (jnp.clip(samples.astype(jnp.float32), -clip_level, clip_level) * widened).astype(jnp.bfloat16)
    slab_rows = cleaned.reshape(CHANNELS, N_TM, SLAB).transpose(1, 0, 2)

    def slab_spectrum(slab_data):
        spectrum = jnp.fft.rfft(slab_data.astype(jnp.float32), n=FFT_LEN, axis=-1)[:, :SLAB]
        return (jnp.real(spectrum).astype(jnp.bfloat16), jnp.imag(spectrum).astype(jnp.bfloat16))
    spec_real, spec_imag = lax.map(slab_spectrum, slab_rows)
    bin_width = min(256, SLAB)
    bin_groups = SLAB // bin_width
    real_groups = spec_real.reshape(N_TM, CHANNELS, bin_groups, bin_width).transpose(2, 0, 1, 3)
    imag_groups = spec_imag.reshape(N_TM, CHANNELS, bin_groups, bin_width).transpose(2, 0, 1, 3)
    group_starts = jnp.arange(bin_groups, dtype=jnp.int32) * bin_width

    def rotate(pieces):
        real_piece, imag_piece, first_bin = pieces
        bin_index = first_bin + jnp.arange(bin_width, dtype=jnp.int32)
        turn_count = delays[:, :, None] * bin_index[None, None, :] % FFT_LEN
        angles = turn_count.astype(jnp.float32) * (2.0 * math.pi / FFT_LEN)
        cos_part = jnp.cos(angles)
        sin_part = jnp.sin(angles)
        real_data = real_piece.astype(jnp.float32)
        imag_data = imag_piece.astype(jnp.float32)
        pattern = 'dck,sck->sdk'
        out_real = jnp.einsum(pattern, cos_part, real_data, precision=highest) + jnp.einsum(pattern, sin_part, imag_data, precision=highest)
        out_imag = jnp.einsum(pattern, cos_part, imag_data, precision=highest) - jnp.einsum(pattern, sin_part, real_data, precision=highest)
        return (out_real, out_imag)
    rot_real, rot_imag = lax.map(rotate, (real_groups, imag_groups, group_starts))
    scale_dm = 1.0 / math.sqrt(CHANNELS)
    rot_real = rot_real.transpose(1, 2, 0, 3).reshape(N_TM, DMS, SLAB) * scale_dm
    rot_imag = rot_imag.transpose(1, 2, 0, 3).reshape(N_TM, DMS, SLAB) * scale_dm
    nyquist = jnp.zeros((N_TM, DMS, 1), jnp.float32)
    combined = lax.complex(jnp.concatenate([rot_real, nyquist], axis=2), jnp.concatenate([rot_imag, nyquist], axis=2))
    padded_out = jnp.fft.irfft(combined, n=FFT_LEN, axis=-1)
    own_part = padded_out[:, :, :SLAB]
    tail_part = padded_out[:, :, SLAB:]
    carried = jnp.concatenate([jnp.zeros((1, DMS, SLAB), padded_out.dtype), tail_part[:-1]], axis=0)
    series = (own_part + carried).transpose(1, 0, 2).reshape(DMS, SAMPLES)
    spectrum = jnp.fft.fft(series, axis=-1)[:, :SEARCH] / math.sqrt(SAMPLES)
    bins_real = lax.optimization_barrier(jnp.real(spectrum).astype(jnp.bfloat16)).astype(jnp.float32)
    bins_imag = lax.optimization_barrier(jnp.imag(spectrum).astype(jnp.bfloat16)).astype(jnp.float32)
    half_taps = TEMPLATE_LEN // 2
    frame_len = SEARCH + TEMPLATE_LEN
    framed = lax.complex(jnp.pad(bins_real, ((0, 0), (half_taps, half_taps))), jnp.pad(bins_imag, ((0, 0), (half_taps, half_taps))))
    kernel = lax.complex(templates[0].astype(jnp.float32), templates[1].astype(jnp.float32))
    reversed_taps = jnp.concatenate([kernel[:, :1], jnp.zeros((TEMPLATES, frame_len - TEMPLATE_LEN), kernel.dtype), kernel[:, :0:-1]], axis=1)
    kernel_spec = jnp.fft.fft(reversed_taps, axis=-1)

    def correlate(frame_row):
        product = jnp.fft.ifft(jnp.fft.fft(frame_row)[None, :] * kernel_spec, axis=-1)[:, :SEARCH]
        return jnp.square(jnp.real(product)) + jnp.square(jnp.imag(product))
    return lax.map(correlate, framed)
```

```python
import math

import jax
import jax.numpy as jnp
from jax import lax
from jax.experimental import pallas as pl
from jax.experimental.pallas import tpu as pltpu
from jax.sharding import PartitionSpec as P

CHANNELS = 1024
SEARCH = 16384
LANES = 128

clip_level = 2.5
highest = lax.Precision.HIGHEST


def counting(length):
    return jnp.arange(length, dtype=jnp.int32)


def phase_table(first_index, second_index, period):
    turn_count = first_index[:, None] * second_index[None, :] % period
    angles = turn_count.astype(jnp.float32) * (2.0 * math.pi / period)
    return (jnp.cos(angles), jnp.sin(angles))


def dedisperse(samples, clip_mask, delays):
    chan_count, slab_len = samples.shape
    rows = slab_len // LANES
    dm_count = delays.shape[0]
    block = 64
    steps = chan_count // block
    padded_len = 2 * slab_len
    scale = 1.0 / math.sqrt(CHANNELS)

    def kernel(delay_ref, sample_ref, mask_ref, out_ref, wrapped_ref, total_ref):
        step = pl.program_id(0)

        @pl.when(step == 0)
        def _():
            total_ref[...] = jnp.zeros_like(total_ref)

        for group in range(block // 16):
            picked = pl.ds(group * 16, 16)
            flags = mask_ref[picked, :].astype(jnp.float32)
            for row in range(rows):
                values = sample_ref[picked, row * LANES : (row + 1) * LANES].astype(jnp.float32)
                values = jnp.clip(values, -clip_level, clip_level) * flags[:, row : row + 1]
                wrapped_ref[picked, row, :] = values
                wrapped_ref[picked, row + rows, :] = values

        lane = lax.broadcasted_iota(jnp.int32, (rows, LANES), 1)
        index = lax.broadcasted_iota(jnp.int32, (rows, LANES), 0) * LANES + lane

        def one_dm(dm, _):
            def one_channel(chan, sums):
                both, own = sums
                delay = delay_ref[dm, step * block + chan]
                high = delay // LANES
                low = delay % LANES
                same = wrapped_ref[chan, pl.ds(rows - high, rows), :]
                before = wrapped_ref[chan, pl.ds(rows - 1 - high, rows), :]
                moved = pltpu.roll(jnp.where(lane < LANES - low, same, before), low, 1)
                return (both + moved, own + jnp.where(index >= delay, moved, 0.0))

            both, own = lax.fori_loop(
                0, block, one_channel, (total_ref[dm, 0], total_ref[dm, 1]), unroll=8
            )
            total_ref[dm, 0] = both
            total_ref[dm, 1] = own
            return 0

        lax.fori_loop(0, dm_count, one_dm, 0)

        @pl.when(step == steps - 1)
        def _():
            sign = (1 - 2 * (lane % 2)).astype(jnp.float32)

            def finish(dm, _):
                both = total_ref[dm, 0]
                own = total_ref[dm, 1]
                half_rate = jnp.sum(both * sign) * sign * (1.0 / padded_len)
                out_ref[dm, :rows, :] = (own - half_rate) * scale
                out_ref[dm, rows:, :] = (both - own - half_rate) * scale
                return 0

            lax.fori_loop(0, dm_count, finish, 0)

    return pl.pallas_call(
        kernel,
        out_shape=jax.ShapeDtypeStruct((dm_count, 2 * rows, LANES), jnp.float32),
        grid_spec=pltpu.PrefetchScalarGridSpec(
            num_scalar_prefetch=1,
            grid=(steps,),
            in_specs=[
                pl.BlockSpec((block, slab_len), lambda i, *_: (i, 0)),
                pl.BlockSpec((block, clip_mask.shape[1]), lambda i, *_: (i, 0)),
            ],
            out_specs=pl.BlockSpec((dm_count, 2 * rows, LANES), lambda i, *_: (0, 0, 0)),
            scratch_shapes=[
                pltpu.VMEM((block, 2 * rows, LANES), jnp.float32),
                pltpu.VMEM((dm_count, 2, rows, LANES), jnp.float32),
            ],
        ),
        compiler_params=pltpu.CompilerParams(vmem_limit_bytes=48 << 20),
    )(delays, samples, clip_mask)


def correlate(framed, templates, bin_count):
    tmpl_count, tap_len = templates.shape[1:]
    blocks = tap_len // LANES
    frame_len = framed.shape[1]
    width = 1024
    steps = bin_count // width

    def kernel(framed_ref, tmpl_ref, out_ref, taps_ref, shifted_ref):
        step = pl.program_id(0)

        @pl.when(step == 0)
        def _():
            row = lax.broadcasted_iota(jnp.int32, (LANES, LANES), 0)
            col = lax.broadcasted_iota(jnp.int32, (LANES, LANES), 1)
            flip = (row + col == LANES - 1).astype(jnp.bfloat16)
            for b in range(blocks):
                cut = slice(b * LANES, (b + 1) * LANES)
                real = jnp.dot(tmpl_ref[0, :, cut], flip, preferred_element_type=jnp.float32)
                imag = jnp.dot(tmpl_ref[1, :, cut], flip, preferred_element_type=jnp.float32)
                taps_ref[b, :tmpl_count, :LANES] = real.astype(jnp.bfloat16)
                taps_ref[b, :tmpl_count, LANES:] = (-imag).astype(jnp.bfloat16)
                taps_ref[b, tmpl_count:, :LANES] = imag.astype(jnp.bfloat16)
                taps_ref[b, tmpl_count:, LANES:] = real.astype(jnp.bfloat16)
            for part in range(2):
                spread = jnp.broadcast_to(framed_ref[part : part + 1, :], (8, frame_len))
                base = pltpu.roll(spread, 0, 1, stride=1, stride_axis=0)
                for g in range(LANES // 16):
                    lower = base if g == 0 else pltpu.roll(base, 16 * g, 1)
                    upper = pltpu.roll(base, 16 * g + 8, 1)
                    start = part * LANES + 16 * g
                    shifted_ref[start : start + 16, :] = jnp.concatenate(
                        [lower, upper], axis=0
                    ).astype(jnp.bfloat16)

        total = jnp.zeros((2 * tmpl_count, width), jnp.float32)
        for b in range(blocks):
            first = pl.multiple_of(step * width + (b + 1) * LANES, LANES)
            total = total + jnp.dot(
                taps_ref[b], shifted_ref[:, pl.ds(first, width)], preferred_element_type=jnp.float32
            )
        out_ref[0] = jnp.square(total[:tmpl_count]) + jnp.square(total[tmpl_count:])

    return pl.pallas_call(
        kernel,
        out_shape=jax.ShapeDtypeStruct((1, tmpl_count, bin_count), jnp.float32),
        grid=(steps,),
        in_specs=[
            pl.BlockSpec((2, frame_len), lambda i: (0, 0)),
            pl.BlockSpec(templates.shape, lambda i: (0, 0, 0)),
        ],
        out_specs=pl.BlockSpec((1, tmpl_count, width), lambda i: (0, 0, i)),
        scratch_shapes=[
            pltpu.VMEM((blocks, 2 * tmpl_count, 2 * LANES), jnp.bfloat16),
            pltpu.VMEM((2 * LANES, frame_len), jnp.bfloat16),
        ],
        compiler_params=pltpu.CompilerParams(vmem_limit_bytes=48 << 20),
    )(framed, templates)


def local(samples, clip_mask, delays, templates):
    partial_value = dedisperse(samples, clip_mask, delays)
    first_bins = partial_value.shape[1]
    half_rows = first_bins // 2
    inner_len = LANES
    owned = lax.all_to_all(partial_value, "tm", split_axis=0, concat_axis=1, tiled=True)
    slab_count = owned.shape[1] // first_bins
    paired = owned.reshape(slab_count, 2, half_rows, inner_len)
    carried = jnp.concatenate(
        [jnp.zeros((1, half_rows, inner_len), jnp.float32), paired[:-1, 1]], axis=0
    )
    series = (paired[:, 0] + carried).reshape(slab_count * half_rows, inner_len)
    whole = lax.psum(series, "band")
    return search(whole, templates)


def search(whole, templates):
    row_count, inner_len = whole.shape
    total_len = row_count * inner_len
    bin_cols = SEARCH // row_count
    scale_bins = 1.0 / math.sqrt(total_len)
    outer_cos, outer_sin = phase_table(counting(row_count), counting(row_count), row_count)
    table_outer = jnp.concatenate([outer_cos, -outer_sin], axis=0)
    hold_cos, hold_sin = phase_table(counting(row_count), counting(inner_len), total_len)
    own_cols = bin_cols // lax.axis_size("band")
    folded = jnp.dot(table_outer, whole, precision=highest)
    fold_real = folded[:row_count]
    fold_imag = folded[row_count:]
    hold_real = fold_real * hold_cos + fold_imag * hold_sin
    hold_imag = fold_imag * hold_cos - fold_real * hold_sin
    half_taps = templates.shape[2] // 2
    side_cols = -(-half_taps // row_count)
    cols = lax.axis_index("band") * own_cols - side_cols + counting(own_cols + 2 * side_cols)
    last_cos, last_sin = phase_table(counting(inner_len), cols % inner_len, inner_len)
    inside = ((cols >= 0) & (cols < bin_cols)).astype(jnp.float32) * scale_bins
    last_cos = last_cos * inside
    last_sin = last_sin * inside
    table_last = jnp.concatenate(
        [
            jnp.concatenate([last_cos, -last_sin], axis=1),
            jnp.concatenate([last_sin, last_cos], axis=1),
        ],
        axis=0,
    )
    out = jnp.dot(jnp.concatenate([hold_real, hold_imag], axis=1), table_last, precision=highest)
    ordered = out.T.reshape(2, -1)
    local_bins = own_cols * row_count
    skip = side_cols * row_count - half_taps
    if skip:
        framed = ordered[:, skip - 1 : skip - 1 + local_bins + 2 * half_taps]
    else:
        framed = jnp.pad(ordered[:, :-1], ((0, 0), (1, 0)))
    return correlate(framed, templates, local_bins)


def solution(mesh):
    in_specs = (P(("beam", "band"), "tm"), P(("beam", "band"), "tm"), P(None, "band"), P())
    out_specs = P(("beam", "tm"), None, "band")
    return jax.shard_map(local, mesh=mesh, in_specs=in_specs, out_specs=out_specs, check_vma=False)
```

```python
import math

import jax
import jax.numpy as jnp
from jax import lax
from jax.experimental import pallas as pl
from jax.experimental.pallas import tpu as pltpu
from jax.sharding import PartitionSpec as P

CHANNELS = 1024
SEARCH = 16384
LANES = 128

clip_level = 2.5
highest = lax.Precision.HIGHEST


def counting(length):
    return jnp.arange(length, dtype=jnp.int32)


def phase_table(first_index, second_index, period):
    turn_count = first_index[:, None] * second_index[None, :] % period
    angles = turn_count.astype(jnp.float32) * (2.0 * math.pi / period)
    return (jnp.cos(angles), jnp.sin(angles))


def dedisperse(samples, clip_mask, delays):
    chan_count, slab_len = samples.shape
    rows = slab_len // LANES
    dm_count = delays.shape[0]
    block = 64
    steps = chan_count // block
    padded_len = 2 * slab_len
    scale = 1.0 / math.sqrt(CHANNELS)
    lane_bits = LANES.bit_length() - 1

    def kernel(delay_ref, sample_ref, mask_ref, out_ref, wrapped_ref, total_ref):
        step = pl.program_id(0)

        @pl.when(step == 0)
        def _():
            total_ref[...] = jnp.zeros_like(total_ref)

        for group in range(block // 16):
            picked = pl.ds(group * 16, 16)
            flags = mask_ref[picked, :].astype(jnp.float32)
            for row in range(rows):
                values = sample_ref[picked, row * LANES : (row + 1) * LANES].astype(jnp.float32)
                values = jnp.clip(values, -clip_level, clip_level) * flags[:, row : row + 1]
                for half in range(2):
                    part = values[8 * half : 8 * half + 8]
                    first = (group * 16 + 8 * half) * 2 * rows + row
                    wrapped_ref[pl.ds(first, 8, stride=2 * rows), :] = part
                    wrapped_ref[pl.ds(first + rows, 8, stride=2 * rows), :] = part

        lane = lax.broadcasted_iota(jnp.int32, (rows, LANES), 1)
        index = lax.broadcasted_iota(jnp.int32, (rows, LANES), 0) * LANES + lane
        from_end = LANES - 1 - lane[:8]

        def one_dm(dm, _):
            chan_base = dm * chan_count + step * block

            def one_channel(chan, sums):
                both, own = sums
                delay = delay_ref[chan_base + chan]
                low = delay & (LANES - 1)
                start = chan * (2 * rows) + (rows - 1) - (delay >> lane_bits)
                keep = from_end >= low
                new_both, new_own = [], []
                for r in range(rows // 8):
                    same = wrapped_ref[pl.ds(start + (1 + 8 * r), 8), :]
                    before = wrapped_ref[pl.ds(start + 8 * r, 8), :]
                    moved = pltpu.roll(jnp.where(keep, same, before), low, 1)
                    new_both.append(both[r] + moved)
                    new_own.append(
                        own[r] + jnp.where(index[8 * r : 8 * r + 8] >= delay, moved, 0.0)
                    )
                return (tuple(new_both), tuple(new_own))

            tiles = [slice(8 * r, 8 * r + 8) for r in range(rows // 8)]
            both, own = lax.fori_loop(
                0,
                block,
                one_channel,
                (
                    tuple(total_ref[dm, 0, t, :] for t in tiles),
                    tuple(total_ref[dm, 1, t, :] for t in tiles),
                ),
                unroll=64,
            )
            for t, x, y in zip(tiles, both, own):
                total_ref[dm, 0, t, :] = x
                total_ref[dm, 1, t, :] = y
            return 0

        lax.fori_loop(0, dm_count, one_dm, 0)

        @pl.when(step == steps - 1)
        def _():
            sign = (1 - 2 * (lane % 2)).astype(jnp.float32)

            def finish(dm, _):
                both = total_ref[dm, 0]
                own = total_ref[dm, 1]
                half_rate = jnp.sum(both * sign) * sign * (1.0 / padded_len)
                out_ref[dm, :rows, :] = ((own - half_rate) * scale).astype(out_ref.dtype)
                out_ref[dm, rows:, :] = ((both - own - half_rate) * scale).astype(out_ref.dtype)
                return 0

            lax.fori_loop(0, dm_count, finish, 0)

    return pl.pallas_call(
        kernel,
        out_shape=jax.ShapeDtypeStruct((dm_count, 2 * rows, LANES), jnp.bfloat16),
        grid_spec=pltpu.PrefetchScalarGridSpec(
            num_scalar_prefetch=1,
            grid=(steps,),
            in_specs=[
                pl.BlockSpec((block, slab_len), lambda i, *_: (i, 0)),
                pl.BlockSpec((block, clip_mask.shape[1]), lambda i, *_: (i, 0)),
            ],
            out_specs=pl.BlockSpec((dm_count, 2 * rows, LANES), lambda i, *_: (0, 0, 0)),
            scratch_shapes=[
                pltpu.VMEM((block * 2 * rows, LANES), jnp.float32),
                pltpu.VMEM((dm_count, 2, rows, LANES), jnp.float32),
            ],
        ),
        compiler_params=pltpu.CompilerParams(vmem_limit_bytes=48 << 20),
    )(delays.reshape(-1), samples, clip_mask)


def gather_series(partial_value):
    tm_count = lax.axis_size("tm")
    band_count = lax.axis_size("band")
    _, padded_rows, _ = partial_value.shape
    rows = padded_rows // 2
    mesh_ids = pl.DeviceIdType.MESH

    def kernel(part_ref, out_ref, held_ref, sent, arrived, passed, received, local_sem):
        me = lax.axis_index("tm")
        band = lax.axis_index("band")

        def device(tm, core):
            return {"tm": tm, "band": core}

        barrier = pltpu.get_barrier_semaphore()
        for k in range(1, tm_count):
            pl.semaphore_signal(
                barrier, 1, device_id=device(lax.rem(me + k, tm_count), band), device_id_type=mesh_ids
            )
        for j in range(1, band_count):
            pl.semaphore_signal(
                barrier, 1, device_id=device(me, lax.rem(band + j, band_count)), device_id_type=mesh_ids
            )
        pl.semaphore_wait(barrier, tm_count + band_count - 2)

        outgoing = []
        for k in range(1, tm_count):
            target = lax.rem(me + k, tm_count)
            copy = pltpu.make_async_remote_copy(
                src_ref=part_ref.at[target],
                dst_ref=held_ref.at[band, me],
                send_sem=sent.at[k],
                recv_sem=arrived.at[k],
                device_id=device(target, band),
                device_id_type=mesh_ids,
            )
            copy.start()
            outgoing.append(copy)
        kept = pltpu.make_async_copy(part_ref.at[me], held_ref.at[band, me], local_sem)
        kept.start()
        handed = []

        def hand_on(source, piece, slot):
            for j in range(1, band_count):
                copy = pltpu.make_async_remote_copy(
                    src_ref=piece,
                    dst_ref=held_ref.at[band, source],
                    send_sem=passed.at[slot, j],
                    recv_sem=received.at[slot, j],
                    device_id=device(me, lax.rem(band + j, band_count)),
                    device_id_type=mesh_ids,
                )
                copy.start()
                handed.append(copy)

        hand_on(me, part_ref.at[me], 0)
        for k in range(1, tm_count):
            outgoing[k - 1].wait_recv()
            source = lax.rem(me + tm_count - k, tm_count)
            hand_on(source, held_ref.at[band, source], k)
        for copy in outgoing:
            copy.wait_send()
        kept.wait()
        for copy in handed:
            copy.wait()

        tail = jnp.zeros((rows, LANES), jnp.float32)
        for s in range(tm_count):
            piece = held_ref[0, s].astype(jnp.float32)
            for b in range(1, band_count):
                piece = piece + held_ref[b, s].astype(jnp.float32)
            out_ref[s * rows : (s + 1) * rows, :] = piece[:rows] + tail
            tail = piece[rows:]

    return pl.pallas_call(
        kernel,
        out_shape=jax.ShapeDtypeStruct((tm_count * rows, LANES), jnp.float32),
        in_specs=[pl.BlockSpec(memory_space=pltpu.VMEM)],
        out_specs=pl.BlockSpec(memory_space=pltpu.VMEM),
        scratch_shapes=[
            pltpu.VMEM((band_count, tm_count, padded_rows, LANES), jnp.bfloat16),
            pltpu.SemaphoreType.DMA((tm_count,)),
            pltpu.SemaphoreType.DMA((tm_count,)),
            pltpu.SemaphoreType.DMA((tm_count, band_count)),
            pltpu.SemaphoreType.DMA((tm_count, band_count)),
            pltpu.SemaphoreType.DMA,
        ],
        compiler_params=pltpu.CompilerParams(collective_id=0, has_side_effects=True),
    )(partial_value)


def correlate(framed, templates, bin_count):
    tmpl_count, tap_len = templates.shape[1:]
    blocks = tap_len // LANES
    frame_len = framed.shape[1]
    width = 1024
    steps = bin_count // width

    def kernel(framed_ref, tmpl_ref, out_ref, taps_ref, shifted_ref):
        step = pl.program_id(0)

        @pl.when(step == 0)
        def _():
            row = lax.broadcasted_iota(jnp.int32, (LANES, LANES), 0)
            col = lax.broadcasted_iota(jnp.int32, (LANES, LANES), 1)
            flip = (row + col == LANES - 1).astype(jnp.bfloat16)
            for b in range(blocks):
                cut = slice(b * LANES, (b + 1) * LANES)
                real = jnp.dot(tmpl_ref[0, :, cut], flip, preferred_element_type=jnp.float32)
                imag = jnp.dot(tmpl_ref[1, :, cut], flip, preferred_element_type=jnp.float32)
                taps_ref[b, :tmpl_count, :LANES] = real.astype(jnp.bfloat16)
                taps_ref[b, :tmpl_count, LANES:] = (-imag).astype(jnp.bfloat16)
                taps_ref[b, tmpl_count:, :LANES] = imag.astype(jnp.bfloat16)
                taps_ref[b, tmpl_count:, LANES:] = real.astype(jnp.bfloat16)
            for part in range(2):
                spread = jnp.broadcast_to(framed_ref[part : part + 1, :], (8, frame_len))
                base = pltpu.roll(spread, 0, 1, stride=1, stride_axis=0)
                for g in range(LANES // 16):
                    lower = base if g == 0 else pltpu.roll(base, 16 * g, 1)
                    upper = pltpu.roll(base, 16 * g + 8, 1)
                    start = part * LANES + 16 * g
                    shifted_ref[start : start + 16, :] = jnp.concatenate(
                        [lower, upper], axis=0
                    ).astype(jnp.bfloat16)

        total = jnp.zeros((2 * tmpl_count, width), jnp.float32)
        for b in range(blocks):
            first = pl.multiple_of(step * width + (b + 1) * LANES, LANES)
            total = total + jnp.dot(
                taps_ref[b], shifted_ref[:, pl.ds(first, width)], preferred_element_type=jnp.float32
            )
        out_ref[0] = jnp.square(total[:tmpl_count]) + jnp.square(total[tmpl_count:])

    return pl.pallas_call(
        kernel,
        out_shape=jax.ShapeDtypeStruct((1, tmpl_count, bin_count), jnp.float32),
        grid=(steps,),
        in_specs=[
            pl.BlockSpec((2, frame_len), lambda i: (0, 0)),
            pl.BlockSpec(templates.shape, lambda i: (0, 0, 0)),
        ],
        out_specs=pl.BlockSpec((1, tmpl_count, width), lambda i: (0, 0, i)),
        scratch_shapes=[
            pltpu.VMEM((blocks, 2 * tmpl_count, 2 * LANES), jnp.bfloat16),
            pltpu.VMEM((2 * LANES, frame_len), jnp.bfloat16),
        ],
        compiler_params=pltpu.CompilerParams(vmem_limit_bytes=48 << 20),
    )(framed, templates)


def local(samples, clip_mask, delays, templates):
    partial_value = dedisperse(samples, clip_mask, delays)
    whole = gather_series(partial_value)
    return search(whole, templates)


def search(whole, templates):
    row_count, inner_len = whole.shape
    total_len = row_count * inner_len
    bin_cols = SEARCH // row_count
    scale_bins = 1.0 / math.sqrt(total_len)
    outer_cos, outer_sin = phase_table(counting(row_count), counting(row_count), row_count)
    table_outer = jnp.concatenate([outer_cos, -outer_sin], axis=0)
    hold_cos, hold_sin = phase_table(counting(row_count), counting(inner_len), total_len)
    own_cols = bin_cols // lax.axis_size("band")
    folded = jnp.dot(table_outer, whole, precision=highest)
    fold_real = folded[:row_count]
    fold_imag = folded[row_count:]
    hold_real = fold_real * hold_cos + fold_imag * hold_sin
    hold_imag = fold_imag * hold_cos - fold_real * hold_sin
    half_taps = templates.shape[2] // 2
    side_cols = -(-half_taps // row_count)
    cols = lax.axis_index("band") * own_cols - side_cols + counting(own_cols + 2 * side_cols)
    last_cos, last_sin = phase_table(counting(inner_len), cols % inner_len, inner_len)
    inside = ((cols >= 0) & (cols < bin_cols)).astype(jnp.float32) * scale_bins
    last_cos = last_cos * inside
    last_sin = last_sin * inside
    table_last = jnp.concatenate(
        [
            jnp.concatenate([last_cos, -last_sin], axis=1),
            jnp.concatenate([last_sin, last_cos], axis=1),
        ],
        axis=0,
    )
    out = jnp.dot(jnp.concatenate([hold_real, hold_imag], axis=1), table_last, precision=highest)
    ordered = out.T.reshape(2, -1)
    local_bins = own_cols * row_count
    skip = side_cols * row_count - half_taps
    if skip:
        framed = ordered[:, skip - 1 : skip - 1 + local_bins + 2 * half_taps]
    else:
        framed = jnp.pad(ordered[:, :-1], ((0, 0), (1, 0)))
    return correlate(framed, templates, local_bins)


def solution(mesh):
    in_specs = (P(("beam", "band"), "tm"), P(("beam", "band"), "tm"), P(None, "band"), P())
    out_specs = P(("beam", "tm"), None, "band")
    return jax.shard_map(local, mesh=mesh, in_specs=in_specs, out_specs=out_specs, check_vma=False)
```

```python
import math

import jax
import jax.numpy as jnp
from jax import lax
from jax.experimental import pallas as pl
from jax.experimental.pallas import tpu as pltpu
from jax.sharding import PartitionSpec as P

CHANNELS = 1024
SEARCH = 16384
LANES = 128

clip_level = 2.5
highest = lax.Precision.HIGHEST


def counting(length):
    return jnp.arange(length, dtype=jnp.int32)


def phase_table(first_index, second_index, period):
    turn_count = first_index[:, None] * second_index[None, :] % period
    angles = turn_count.astype(jnp.float32) * (2.0 * math.pi / period)
    return (jnp.cos(angles), jnp.sin(angles))


def dedisperse(samples, clip_mask, delays):
    chan_count, slab_len = samples.shape
    rows = slab_len // LANES
    dm_count = delays.shape[0]
    block = 128
    steps = chan_count // block
    padded_len = 2 * slab_len
    scale = 1.0 / math.sqrt(CHANNELS)
    assert clip_mask.shape[1] == rows
    lane_bits = LANES.bit_length() - 1

    def kernel(delay_ref, sample_ref, mask_ref, out_ref, wrapped_ref, total_ref):
        step = pl.program_id(0)

        @pl.when(step == 0)
        def _():
            total_ref[...] = jnp.zeros_like(total_ref)

        flags = mask_ref[...]
        for chan in range(block):
            values = jnp.clip(sample_ref[chan].astype(jnp.float32), -clip_level, clip_level)
            values = values * flags[:, chan : chan + 1]
            wrapped_ref[chan * 2 * rows : chan * 2 * rows + rows, :] = values
            wrapped_ref[chan * 2 * rows + rows : (chan + 1) * 2 * rows, :] = values

        lane = lax.broadcasted_iota(jnp.int32, (rows, LANES), 1)
        index = lax.broadcasted_iota(jnp.int32, (rows, LANES), 0) * LANES + lane
        from_end = LANES - 1 - lane[:16]

        def one_dm(dm, _):
            chan_base = dm * chan_count + step * block

            def one_channel(chan, sums):
                both, own = sums
                delay = delay_ref[chan_base + chan]
                low = delay & (LANES - 1)
                start = chan * (2 * rows) + (rows - 1) - (delay >> lane_bits)
                keep = from_end >= low
                new_both, new_own = [], []
                before = wrapped_ref[pl.ds(start, rows), :]
                same = wrapped_ref[pl.ds(start + 1, rows), :]
                for r in range(rows // 16):
                    pair = slice(16 * r, 16 * r + 16)
                    merged = jnp.where(keep, same[pair], before[pair]).astype(jnp.bfloat16)
                    rolled = pltpu.roll(merged, low, 1).astype(jnp.float32)
                    for h in range(2):
                        moved = rolled[8 * h : 8 * h + 8]
                        t = 2 * r + h
                        new_both.append(both[t] + moved)
                        new_own.append(
                            own[t] + jnp.where(index[8 * t : 8 * t + 8] >= delay, moved, 0.0)
                        )
                return (tuple(new_both), tuple(new_own))

            tiles = [slice(8 * r, 8 * r + 8) for r in range(rows // 8)]
            both, own = lax.fori_loop(
                0,
                block,
                one_channel,
                (
                    tuple(total_ref[dm, 0, t, :] for t in tiles),
                    tuple(total_ref[dm, 1, t, :] for t in tiles),
                ),
                unroll=64,
            )
            for t, x, y in zip(tiles, both, own):
                total_ref[dm, 0, t, :] = x
                total_ref[dm, 1, t, :] = y
            return 0

        lax.fori_loop(0, dm_count, one_dm, 0)

        @pl.when(step == steps - 1)
        def _():
            sign = (1 - 2 * (lane % 2)).astype(jnp.float32)

            def finish(dm, _):
                both = total_ref[dm, 0]
                own = total_ref[dm, 1]
                half_rate = jnp.sum(both * sign) * sign * (1.0 / padded_len)
                out_ref[dm, :rows, :] = ((own - half_rate) * scale).astype(out_ref.dtype)
                out_ref[dm, rows:, :] = ((both - own - half_rate) * scale).astype(out_ref.dtype)
                return 0

            lax.fori_loop(0, dm_count, finish, 0)

    return pl.pallas_call(
        kernel,
        out_shape=jax.ShapeDtypeStruct((dm_count, 2 * rows, LANES), jnp.bfloat16),
        grid_spec=pltpu.PrefetchScalarGridSpec(
            num_scalar_prefetch=1,
            grid=(steps,),
            in_specs=[
                pl.BlockSpec((block, rows, LANES), lambda i, *_: (i, 0, 0)),
                pl.BlockSpec((rows, block), lambda i, *_: (0, i)),
            ],
            out_specs=pl.BlockSpec((dm_count, 2 * rows, LANES), lambda i, *_: (0, 0, 0)),
            scratch_shapes=[
                pltpu.VMEM((block * 2 * rows, LANES), jnp.float32),
                pltpu.VMEM((dm_count, 2, rows, LANES), jnp.float32),
            ],
        ),
        compiler_params=pltpu.CompilerParams(vmem_limit_bytes=48 << 20),
    )(
        delays.reshape(-1),
        samples.reshape(chan_count, rows, LANES),
        clip_mask.T.astype(jnp.float32),
    )


def gather_series(partial_value):
    tm_count = lax.axis_size("tm")
    band_count = lax.axis_size("band")
    _, padded_rows, _ = partial_value.shape
    rows = padded_rows // 2
    mesh_ids = pl.DeviceIdType.MESH

    def kernel(part_ref, out_ref, held_ref, sent, arrived, passed, received, local_sem):
        me = lax.axis_index("tm")
        band = lax.axis_index("band")

        def device(tm, core):
            return {"tm": tm, "band": core}

        barrier = pltpu.get_barrier_semaphore()
        for k in range(1, tm_count):
            pl.semaphore_signal(
                barrier, 1, device_id=device(lax.rem(me + k, tm_count), band), device_id_type=mesh_ids
            )
        for j in range(1, band_count):
            pl.semaphore_signal(
                barrier, 1, device_id=device(me, lax.rem(band + j, band_count)), device_id_type=mesh_ids
            )
        pl.semaphore_wait(barrier, tm_count + band_count - 2)

        outgoing = []
        for k in range(1, tm_count):
            target = lax.rem(me + k, tm_count)
            copy = pltpu.make_async_remote_copy(
                src_ref=part_ref.at[target],
                dst_ref=held_ref.at[band, me],
                send_sem=sent.at[k],
                recv_sem=arrived.at[k],
                device_id=device(target, band),
                device_id_type=mesh_ids,
            )
            copy.start()
            outgoing.append(copy)
        kept = pltpu.make_async_copy(part_ref.at[me], held_ref.at[band, me], local_sem)
        kept.start()
        handed = []

        def hand_on(source, piece, slot):
            for j in range(1, band_count):
                copy = pltpu.make_async_remote_copy(
                    src_ref=piece,
                    dst_ref=held_ref.at[band, source],
                    send_sem=passed.at[slot, j],
                    recv_sem=received.at[slot, j],
                    device_id=device(me, lax.rem(band + j, band_count)),
                    device_id_type=mesh_ids,
                )
                copy.start()
                handed.append(copy)

        hand_on(me, part_ref.at[me], 0)
        for k in range(1, tm_count):
            outgoing[k - 1].wait_recv()
            source = lax.rem(me + tm_count - k, tm_count)
            hand_on(source, held_ref.at[band, source], k)
        for copy in outgoing:
            copy.wait_send()
        kept.wait()
        for copy in handed:
            copy.wait()

        tail = jnp.zeros((rows, LANES), jnp.float32)
        for s in range(tm_count):
            piece = held_ref[0, s].astype(jnp.float32)
            for b in range(1, band_count):
                piece = piece + held_ref[b, s].astype(jnp.float32)
            out_ref[s * rows : (s + 1) * rows, :] = piece[:rows] + tail
            tail = piece[rows:]

    return pl.pallas_call(
        kernel,
        out_shape=jax.ShapeDtypeStruct((tm_count * rows, LANES), jnp.float32),
        in_specs=[pl.BlockSpec(memory_space=pltpu.VMEM)],
        out_specs=pl.BlockSpec(memory_space=pltpu.VMEM),
        scratch_shapes=[
            pltpu.VMEM((band_count, tm_count, padded_rows, LANES), jnp.bfloat16),
            pltpu.SemaphoreType.DMA((tm_count,)),
            pltpu.SemaphoreType.DMA((tm_count,)),
            pltpu.SemaphoreType.DMA((tm_count, band_count)),
            pltpu.SemaphoreType.DMA((tm_count, band_count)),
            pltpu.SemaphoreType.DMA,
        ],
        compiler_params=pltpu.CompilerParams(collective_id=0, has_side_effects=True),
    )(partial_value)


def correlate(framed, templates, bin_count):
    tmpl_count, tap_len = templates.shape[1:]
    blocks = tap_len // LANES
    frame_len = framed.shape[1]
    width = 1024
    steps = bin_count // width

    def kernel(framed_ref, tmpl_ref, out_ref, taps_ref, shifted_ref):
        step = pl.program_id(0)

        @pl.when(step == 0)
        def _():
            row = lax.broadcasted_iota(jnp.int32, (LANES, LANES), 0)
            col = lax.broadcasted_iota(jnp.int32, (LANES, LANES), 1)
            flip = (row + col == LANES - 1).astype(jnp.bfloat16)
            for b in range(blocks):
                cut = slice(b * LANES, (b + 1) * LANES)
                real = jnp.dot(tmpl_ref[0, :, cut], flip, preferred_element_type=jnp.float32)
                imag = jnp.dot(tmpl_ref[1, :, cut], flip, preferred_element_type=jnp.float32)
                taps_ref[b, :tmpl_count, :LANES] = real.astype(jnp.bfloat16)
                taps_ref[b, :tmpl_count, LANES:] = (-imag).astype(jnp.bfloat16)
                taps_ref[b, tmpl_count:, :LANES] = imag.astype(jnp.bfloat16)
                taps_ref[b, tmpl_count:, LANES:] = real.astype(jnp.bfloat16)
            for part in range(2):
                spread = jnp.broadcast_to(framed_ref[part : part + 1, :], (8, frame_len))
                base = pltpu.roll(spread, 0, 1, stride=1, stride_axis=0)
                for g in range(LANES // 16):
                    lower = base if g == 0 else pltpu.roll(base, 16 * g, 1)
                    upper = pltpu.roll(base, 16 * g + 8, 1)
                    start = part * LANES + 16 * g
                    shifted_ref[start : start + 16, :] = jnp.concatenate(
                        [lower, upper], axis=0
                    ).astype(jnp.bfloat16)

        total = jnp.zeros((2 * tmpl_count, width), jnp.float32)
        for b in range(blocks):
            first = pl.multiple_of(step * width + (b + 1) * LANES, LANES)
            total = total + jnp.dot(
                taps_ref[b], shifted_ref[:, pl.ds(first, width)], preferred_element_type=jnp.float32
            )
        out_ref[0] = jnp.square(total[:tmpl_count]) + jnp.square(total[tmpl_count:])

    return pl.pallas_call(
        kernel,
        out_shape=jax.ShapeDtypeStruct((1, tmpl_count, bin_count), jnp.float32),
        grid=(steps,),
        in_specs=[
            pl.BlockSpec((2, frame_len), lambda i: (0, 0)),
            pl.BlockSpec(templates.shape, lambda i: (0, 0, 0)),
        ],
        out_specs=pl.BlockSpec((1, tmpl_count, width), lambda i: (0, 0, i)),
        scratch_shapes=[
            pltpu.VMEM((blocks, 2 * tmpl_count, 2 * LANES), jnp.bfloat16),
            pltpu.VMEM((2 * LANES, frame_len), jnp.bfloat16),
        ],
        compiler_params=pltpu.CompilerParams(vmem_limit_bytes=48 << 20),
    )(framed, templates)


def local(samples, clip_mask, delays, templates):
    partial_value = dedisperse(samples, clip_mask, delays)
    whole = gather_series(partial_value)
    return search(whole, templates)


def search(whole, templates):
    row_count, inner_len = whole.shape
    total_len = row_count * inner_len
    bin_cols = SEARCH // row_count
    scale_bins = 1.0 / math.sqrt(total_len)
    outer_cos, outer_sin = phase_table(counting(row_count), counting(row_count), row_count)
    table_outer = jnp.concatenate([outer_cos, -outer_sin], axis=0)
    hold_cos, hold_sin = phase_table(counting(row_count), counting(inner_len), total_len)
    own_cols = bin_cols // lax.axis_size("band")
    folded = jnp.dot(table_outer, whole, precision=highest)
    fold_real = folded[:row_count]
    fold_imag = folded[row_count:]
    hold_real = fold_real * hold_cos + fold_imag * hold_sin
    hold_imag = fold_imag * hold_cos - fold_real * hold_sin
    half_taps = templates.shape[2] // 2
    side_cols = -(-half_taps // row_count)
    cols = lax.axis_index("band") * own_cols - side_cols + counting(own_cols + 2 * side_cols)
    last_cos, last_sin = phase_table(counting(inner_len), cols % inner_len, inner_len)
    inside = ((cols >= 0) & (cols < bin_cols)).astype(jnp.float32) * scale_bins
    last_cos = last_cos * inside
    last_sin = last_sin * inside
    table_last = jnp.concatenate(
        [
            jnp.concatenate([last_cos, -last_sin], axis=1),
            jnp.concatenate([last_sin, last_cos], axis=1),
        ],
        axis=0,
    )
    out = jnp.dot(jnp.concatenate([hold_real, hold_imag], axis=1), table_last, precision=highest)
    ordered = out.T.reshape(2, -1)
    local_bins = own_cols * row_count
    skip = side_cols * row_count - half_taps
    if skip:
        framed = ordered[:, skip - 1 : skip - 1 + local_bins + 2 * half_taps]
    else:
        framed = jnp.pad(ordered[:, :-1], ((0, 0), (1, 0)))
    return correlate(framed, templates, local_bins)


def solution(mesh):
    in_specs = (P(("beam", "band"), "tm"), P(("beam", "band"), "tm"), P(None, "band"), P())
    out_specs = P(("beam", "tm"), None, "band")
    return jax.shard_map(local, mesh=mesh, in_specs=in_specs, out_specs=out_specs, check_vma=False)
```

```python
import math

import jax
import jax.numpy as jnp
from jax import lax
from jax.experimental import pallas as pl
from jax.experimental.pallas import tpu as pltpu
from jax.sharding import PartitionSpec as P

CHANNELS = 1024
SEARCH = 16384
LANES = 128

clip_level = 2.5
fine = lax.Precision.HIGH


def counting(length):
    return jnp.arange(length, dtype=jnp.int32)


def phase_table(first_index, second_index, period):
    turn_count = first_index[:, None] * second_index[None, :] % period
    angles = turn_count.astype(jnp.float32) * (2.0 * math.pi / period)
    return (jnp.cos(angles), jnp.sin(angles))


def dedisperse(samples, clip_mask, delays):
    chan_count, slab_len = samples.shape
    rows = slab_len // LANES
    dm_count = delays.shape[0]
    block = 128
    steps = chan_count // block
    padded_len = 2 * slab_len
    scale = 1.0 / math.sqrt(CHANNELS)
    assert clip_mask.shape[1] == rows
    lane_bits = LANES.bit_length() - 1

    def kernel(delay_ref, sample_ref, mask_ref, out_ref, wrapped_ref, total_ref):
        step = pl.program_id(0)

        @pl.when(step == 0)
        def _():
            total_ref[...] = jnp.zeros_like(total_ref)

        flags = mask_ref[...]
        for chan in range(block):
            values = jnp.clip(sample_ref[chan].astype(jnp.float32), -clip_level, clip_level)
            values = values * flags[:, chan : chan + 1]
            wrapped_ref[chan * 2 * rows : chan * 2 * rows + rows, :] = values
            wrapped_ref[chan * 2 * rows + rows : (chan + 1) * 2 * rows, :] = values

        lane = lax.broadcasted_iota(jnp.int32, (rows, LANES), 1)
        index = lax.broadcasted_iota(jnp.int32, (rows, LANES), 0) * LANES + lane
        from_end = LANES - 1 - lane[:16]

        def one_dm(dm, _):
            chan_base = dm * chan_count + step * block

            def one_channel(chan, sums):
                both, own = sums
                delay = delay_ref[chan_base + chan]
                low = delay & (LANES - 1)
                start = chan * (2 * rows) + (rows - 1) - (delay >> lane_bits)
                keep = from_end >= low
                new_both, new_own = [], []
                before = wrapped_ref[pl.ds(start, rows), :]
                same = wrapped_ref[pl.ds(start + 1, rows), :]
                for r in range(rows // 16):
                    pair = slice(16 * r, 16 * r + 16)
                    merged = jnp.where(keep, same[pair], before[pair]).astype(jnp.bfloat16)
                    rolled = pltpu.roll(merged, low, 1).astype(jnp.float32)
                    for h in range(2):
                        moved = rolled[8 * h : 8 * h + 8]
                        t = 2 * r + h
                        new_both.append(both[t] + moved)
                        new_own.append(
                            own[t] + jnp.where(index[8 * t : 8 * t + 8] >= delay, moved, 0.0)
                        )
                return (tuple(new_both), tuple(new_own))

            tiles = [slice(8 * r, 8 * r + 8) for r in range(rows // 8)]
            both, own = lax.fori_loop(
                0,
                block,
                one_channel,
                (
                    tuple(total_ref[dm, 0, t, :] for t in tiles),
                    tuple(total_ref[dm, 1, t, :] for t in tiles),
                ),
                unroll=block,
            )
            for t, x, y in zip(tiles, both, own):
                total_ref[dm, 0, t, :] = x
                total_ref[dm, 1, t, :] = y
            return 0

        lax.fori_loop(0, dm_count, one_dm, 0)

        @pl.when(step == steps - 1)
        def _():
            sign = (1 - 2 * (lane % 2)).astype(jnp.float32)

            def finish(dm, _):
                both = total_ref[dm, 0]
                own = total_ref[dm, 1]
                half_rate = jnp.sum(both * sign) * sign * (1.0 / padded_len)
                out_ref[dm, :rows, :] = ((own - half_rate) * scale).astype(out_ref.dtype)
                out_ref[dm, rows:, :] = ((both - own - half_rate) * scale).astype(out_ref.dtype)
                return 0

            lax.fori_loop(0, dm_count, finish, 0)

    return pl.pallas_call(
        kernel,
        out_shape=jax.ShapeDtypeStruct((dm_count, 2 * rows, LANES), jnp.bfloat16),
        grid_spec=pltpu.PrefetchScalarGridSpec(
            num_scalar_prefetch=1,
            grid=(steps,),
            in_specs=[
                pl.BlockSpec((block, rows, LANES), lambda i, *_: (i, 0, 0)),
                pl.BlockSpec((rows, block), lambda i, *_: (0, i)),
            ],
            out_specs=pl.BlockSpec((dm_count, 2 * rows, LANES), lambda i, *_: (0, 0, 0)),
            scratch_shapes=[
                pltpu.VMEM((block * 2 * rows, LANES), jnp.float32),
                pltpu.VMEM((dm_count, 2, rows, LANES), jnp.float32),
            ],
        ),
        compiler_params=pltpu.CompilerParams(vmem_limit_bytes=48 << 20),
    )(
        delays.reshape(-1),
        samples.reshape(chan_count, rows, LANES),
        clip_mask.T.astype(jnp.float32),
    )


def gather_series(partial_value):
    tm_count = lax.axis_size("tm")
    band_count = lax.axis_size("band")
    _, padded_rows, _ = partial_value.shape
    rows = padded_rows // 2
    mesh_ids = pl.DeviceIdType.MESH

    def kernel(part_ref, out_ref, held_ref, sent, arrived, passed, received, local_sem):
        me = lax.axis_index("tm")
        band = lax.axis_index("band")

        def device(tm, core):
            return {"tm": tm, "band": core}

        barrier = pltpu.get_barrier_semaphore()
        for k in range(1, tm_count):
            pl.semaphore_signal(
                barrier, 1, device_id=device(lax.rem(me + k, tm_count), band), device_id_type=mesh_ids
            )
        for j in range(1, band_count):
            pl.semaphore_signal(
                barrier, 1, device_id=device(me, lax.rem(band + j, band_count)), device_id_type=mesh_ids
            )
        pl.semaphore_wait(barrier, tm_count + band_count - 2)

        outgoing = []
        for k in range(1, tm_count):
            target = lax.rem(me + k, tm_count)
            copy = pltpu.make_async_remote_copy(
                src_ref=part_ref.at[target],
                dst_ref=held_ref.at[band, me],
                send_sem=sent.at[k],
                recv_sem=arrived.at[k],
                device_id=device(target, band),
                device_id_type=mesh_ids,
            )
            copy.start()
            outgoing.append(copy)
        kept = pltpu.make_async_copy(part_ref.at[me], held_ref.at[band, me], local_sem)
        kept.start()
        handed = []

        def hand_on(source, piece, slot):
            for j in range(1, band_count):
                copy = pltpu.make_async_remote_copy(
                    src_ref=piece,
                    dst_ref=held_ref.at[band, source],
                    send_sem=passed.at[slot, j],
                    recv_sem=received.at[slot, j],
                    device_id=device(me, lax.rem(band + j, band_count)),
                    device_id_type=mesh_ids,
                )
                copy.start()
                handed.append(copy)

        hand_on(me, part_ref.at[me], 0)
        for k in range(1, tm_count):
            outgoing[k - 1].wait_recv()
            source = lax.rem(me + tm_count - k, tm_count)
            hand_on(source, held_ref.at[band, source], k)
        for copy in outgoing:
            copy.wait_send()
        kept.wait()
        for copy in handed:
            copy.wait()

        tail = jnp.zeros((rows, LANES), jnp.float32)
        for s in range(tm_count):
            piece = held_ref[0, s].astype(jnp.float32)
            for b in range(1, band_count):
                piece = piece + held_ref[b, s].astype(jnp.float32)
            out_ref[s * rows : (s + 1) * rows, :] = piece[:rows] + tail
            tail = piece[rows:]

    return pl.pallas_call(
        kernel,
        out_shape=jax.ShapeDtypeStruct((tm_count * rows, LANES), jnp.float32),
        in_specs=[pl.BlockSpec(memory_space=pltpu.VMEM)],
        out_specs=pl.BlockSpec(memory_space=pltpu.VMEM),
        scratch_shapes=[
            pltpu.VMEM((band_count, tm_count, padded_rows, LANES), jnp.bfloat16),
            pltpu.SemaphoreType.DMA((tm_count,)),
            pltpu.SemaphoreType.DMA((tm_count,)),
            pltpu.SemaphoreType.DMA((tm_count, band_count)),
            pltpu.SemaphoreType.DMA((tm_count, band_count)),
            pltpu.SemaphoreType.DMA,
        ],
        compiler_params=pltpu.CompilerParams(collective_id=0, has_side_effects=True),
    )(partial_value)


def correlate(framed, templates, bin_count):
    tmpl_count, tap_len = templates.shape[1:]
    blocks = tap_len // LANES
    frame_len = framed.shape[1]
    width = 1024
    steps = bin_count // width

    def kernel(framed_ref, tmpl_ref, out_ref, taps_ref, shifted_ref):
        step = pl.program_id(0)

        @pl.when(step == 0)
        def _():
            row = lax.broadcasted_iota(jnp.int32, (LANES, LANES), 0)
            col = lax.broadcasted_iota(jnp.int32, (LANES, LANES), 1)
            flip = (row + col == LANES - 1).astype(jnp.bfloat16)
            for b in range(blocks):
                cut = slice(b * LANES, (b + 1) * LANES)
                real = jnp.dot(tmpl_ref[0, :, cut], flip, preferred_element_type=jnp.float32)
                imag = jnp.dot(tmpl_ref[1, :, cut], flip, preferred_element_type=jnp.float32)
                taps_ref[b, :tmpl_count, :LANES] = real.astype(jnp.bfloat16)
                taps_ref[b, :tmpl_count, LANES:] = (-imag).astype(jnp.bfloat16)
                taps_ref[b, tmpl_count:, :LANES] = imag.astype(jnp.bfloat16)
                taps_ref[b, tmpl_count:, LANES:] = real.astype(jnp.bfloat16)
            for part in range(2):
                spread = jnp.broadcast_to(framed_ref[part : part + 1, :], (8, frame_len))
                base = pltpu.roll(spread, 0, 1, stride=1, stride_axis=0)
                for g in range(LANES // 16):
                    lower = base if g == 0 else pltpu.roll(base, 16 * g, 1)
                    upper = pltpu.roll(base, 16 * g + 8, 1)
                    start = part * LANES + 16 * g
                    shifted_ref[start : start + 16, :] = jnp.concatenate(
                        [lower, upper], axis=0
                    ).astype(jnp.bfloat16)

        total = jnp.zeros((2 * tmpl_count, width), jnp.float32)
        for b in range(blocks):
            first = pl.multiple_of(step * width + (b + 1) * LANES, LANES)
            total = total + jnp.dot(
                taps_ref[b], shifted_ref[:, pl.ds(first, width)], preferred_element_type=jnp.float32
            )
        out_ref[0] = jnp.square(total[:tmpl_count]) + jnp.square(total[tmpl_count:])

    return pl.pallas_call(
        kernel,
        out_shape=jax.ShapeDtypeStruct((1, tmpl_count, bin_count), jnp.float32),
        grid=(steps,),
        in_specs=[
            pl.BlockSpec((2, frame_len), lambda i: (0, 0)),
            pl.BlockSpec(templates.shape, lambda i: (0, 0, 0)),
        ],
        out_specs=pl.BlockSpec((1, tmpl_count, width), lambda i: (0, 0, i)),
        scratch_shapes=[
            pltpu.VMEM((blocks, 2 * tmpl_count, 2 * LANES), jnp.bfloat16),
            pltpu.VMEM((2 * LANES, frame_len), jnp.bfloat16),
        ],
        compiler_params=pltpu.CompilerParams(vmem_limit_bytes=48 << 20),
    )(framed, templates)


def local(samples, clip_mask, delays, templates):
    partial_value = dedisperse(samples, clip_mask, delays)
    whole = gather_series(partial_value)
    return search(whole, templates)


def search(whole, templates):
    row_count, inner_len = whole.shape
    total_len = row_count * inner_len
    bin_cols = SEARCH // row_count
    scale_bins = 1.0 / math.sqrt(total_len)
    outer_cos, outer_sin = phase_table(counting(row_count), counting(row_count), row_count)
    table_outer = jnp.concatenate([outer_cos, -outer_sin], axis=0)
    hold_cos, hold_sin = phase_table(counting(row_count), counting(inner_len), total_len)
    own_cols = bin_cols // lax.axis_size("band")
    folded = jnp.dot(table_outer, whole, precision=fine)
    fold_real = folded[:row_count]
    fold_imag = folded[row_count:]
    hold_real = fold_real * hold_cos + fold_imag * hold_sin
    hold_imag = fold_imag * hold_cos - fold_real * hold_sin
    half_taps = templates.shape[2] // 2
    side_cols = -(-half_taps // row_count)
    cols = lax.axis_index("band") * own_cols - side_cols + counting(own_cols + 2 * side_cols)
    last_cos, last_sin = phase_table(counting(inner_len), cols % inner_len, inner_len)
    inside = ((cols >= 0) & (cols < bin_cols)).astype(jnp.float32) * scale_bins
    last_cos = last_cos * inside
    last_sin = last_sin * inside
    table_last = jnp.concatenate(
        [
            jnp.concatenate([last_cos, -last_sin], axis=1),
            jnp.concatenate([last_sin, last_cos], axis=1),
        ],
        axis=0,
    )
    out = jnp.dot(jnp.concatenate([hold_real, hold_imag], axis=1), table_last, precision=fine)
    ordered = out.T.reshape(2, -1)
    local_bins = own_cols * row_count
    skip = side_cols * row_count - half_taps
    if skip:
        framed = ordered[:, skip - 1 : skip - 1 + local_bins + 2 * half_taps]
    else:
        framed = jnp.pad(ordered[:, :-1], ((0, 0), (1, 0)))
    return correlate(framed, templates, local_bins)


def solution(mesh):
    in_specs = (P(("beam", "band"), "tm"), P(("beam", "band"), "tm"), P(None, "band"), P())
    out_specs = P(("beam", "tm"), None, "band")
    return jax.shard_map(local, mesh=mesh, in_specs=in_specs, out_specs=out_specs, check_vma=False)
```
